32 devices in a mesh: batch: 4 (over y, x), seq: 8 (over z, core).
Axes of the slice: x: 2, y: 2, z: 4, core: 2. Of those that a mesh axis runs over, the one named last changes fastest.
Arguments:
- hidden: float32 [8192, 1024], P(('batch', 'seq')), may hold values from -6 to 6
- cotangent: float32 [8192, 1024], P(('batch', 'seq')), may hold values from -6 to 6
- norm_gain: bfloat16 [2, 1024], P(None, ('batch', 'seq')), may hold values from 0.099609375 to 1.8984375
- in_proj: bfloat16 [2, 1024, 4384], P(None, ('batch', 'seq')), may hold values from -0.1875 to 0.1875
- conv_weight: bfloat16 [2, 4, 2304], P(None, None, ('batch', 'seq')), may hold values from -3 to 3
- conv_bias: bfloat16 [2, 2304], P(None, ('batch', 'seq')), may hold values from -3 to 3
- dt_bias: float32 [2, 32], P(None, 'seq'), may hold values from -6 to -1
- a_log: float32 [2, 32], P(None, 'seq'), may hold values from -1.5 to 2.5
- d_skip: float32 [2, 32], P(None, 'seq'), may hold values from 0.5 to 1.5
- gate_gain: bfloat16 [2, 2048], P(None, ('batch', 'seq')), may hold values from 0.099609375 to 1.8984375
- out_proj: bfloat16 [2, 2048, 1024], P(None, ('batch', 'seq')), may hold values from -0.125 to 0.125
Outputs:
- output: float32 [8192, 1024], P(('batch', 'seq'))
- grad_hidden: float32 [8192, 1024], P(('batch', 'seq'))
- grad_norm_gain: float32 [2, 1024], P(None, ('batch', 'seq'))
- grad_in_proj: float32 [2, 1024, 4384], P(None, ('batch', 'seq'))
- grad_conv_weight: float32 [2, 4, 2304], P(None, None, ('batch', 'seq'))
- grad_conv_bias: float32 [2, 2304], P(None, ('batch', 'seq'))
- grad_dt_bias: float32 [2, 32], P(None, 'seq')
- grad_a_log: float32 [2, 32], P(None, 'seq')
- grad_d_skip: float32 [2, 32], P(None, 'seq')
- grad_gate_gain: float32 [2, 2048], P(None, ('batch', 'seq'))
- grad_out_proj: float32 [2, 2048, 1024], P(None, ('batch', 'seq'))
The draws below stay inside these ranges and needn't reach their ends.
All inputs are finite; a program needn't handle non-finite values.
Results may differ from the reference program's by a relative error of at most 0.023.
Values may be sent and summed in bfloat16 or wider, within the bound.
No kernel may reach another device: no remote copies, remote signals or barrier semaphores. Data moves between devices by JAX's collectives and lax.ppermute only.
A program may use at most 320 MiB of HBM per device.

```python
import jax
import jax.numpy as jnp
from jax import lax

D = 1024
HEADS = 32
STATE = 128
CONV = 4
SPAN = 256
SEQLEN = 2048
LAYERS = 2
INNER = 2048
CONV_CH = 2304
PROJ = 4384
TOKENS = 8192
SEQS = 4


def shard_levels(stream_key, extent, shards, low, high):
    def one(dim, shards_of):
        heights = jax.random.uniform(jax.random.fold_in(jax.random.fold_in(stream_key, 6), dim), (shards_of,), jnp.float32, low / len(shards), high / len(shards))
        return jnp.repeat(jnp.exp(heights), extent[dim] // shards_of).reshape((-1,) + (1,) * (len(extent) - dim - 1))

    level = one(*shards[0])
    for cut in shards[1:]:
        level = level * one(*cut)
    return level


def scatter_about(rng, dims, scale, reach, split=(), dtype=jnp.bfloat16):
    entries = jax.random.normal(rng, dims, jnp.float32) * scale
    if len(split) > 0:
        entries = shard_levels(rng, dims, split, -0.22, 0.18) * entries
    return jnp.clip(entries, min=-reach, max=reach).astype(dtype)


def setup_inputs(seed: int = 0) -> dict:
    arg_keys = jax.random.split(jax.random.key(seed), 12)
    return {
        "hidden": scatter_about(arg_keys[0], (TOKENS, D), 1.0, 6.0, ((0, 32),), jnp.float32),
        "cotangent": scatter_about(arg_keys[1], (TOKENS, D), 1.0, 6.0, ((0, 32),), jnp.float32),
        "norm_gain": jnp.clip(1.0 + 0.18 * jax.random.normal(arg_keys[2], (LAYERS, D), jnp.float32), 0.099609375, 1.8984375).astype(jnp.bfloat16),
        "in_proj": scatter_about(arg_keys[3], (LAYERS, D, PROJ), D ** -0.5, 0.1875, ((1, 32),)),
        "conv_weight": scatter_about(arg_keys[4], (LAYERS, CONV, CONV_CH), CONV ** -0.5, 3.0, ((2, 32),)),
        "conv_bias": scatter_about(arg_keys[5], (LAYERS, CONV_CH), 0.5, 3.0, ((1, 32),)),
        "dt_bias": jnp.clip(-6.0 + 5.0 * jax.random.uniform(arg_keys[6], (LAYERS, HEADS), jnp.float32) ** shard_levels(arg_keys[6], (LAYERS, HEADS), ((1, 8),), -0.2, 0.2), -6.0, -1.0),
        "a_log": jnp.clip(-1.5 + 4.0 * jax.random.uniform(arg_keys[7], (LAYERS, HEADS), jnp.float32) ** shard_levels(arg_keys[7], (LAYERS, HEADS), ((1, 8),), -0.2, 0.2), -1.5, 2.5),
        "d_skip": jnp.clip(0.5 + 1.0 * jax.random.uniform(arg_keys[8], (LAYERS, HEADS), jnp.float32) ** shard_levels(arg_keys[8], (LAYERS, HEADS), ((1, 8),), -0.2, 0.2), 0.5, 1.5),
        "gate_gain": jnp.clip(1.0 + 0.18 * jax.random.normal(arg_keys[9], (LAYERS, INNER), jnp.float32), 0.099609375, 1.8984375).astype(jnp.bfloat16),
        "out_proj": scatter_about(arg_keys[10], (LAYERS, INNER, D), INNER ** -0.5, 0.125, ((1, 32),)),
    }


EPS = 1e-05
HIGHEST = lax.Precision.HIGHEST

def row_norm(rows, gain):
    factor = lax.rsqrt(lax.optimization_barrier(jnp.mean(rows * rows, axis=-1, keepdims=True)) + EPS)
    return rows * factor * gain

def causal_conv(signal, kernel, offset):
    taps = kernel.shape[0]
    length = signal.shape[0]
    padded = jnp.pad(signal, ((taps - 1, 0), (0, 0)))
    summed = offset + jnp.zeros_like(signal)
    for k in range(taps):
        summed = summed + kernel[k] * padded[k:k + length]
    return jax.nn.silu(summed)

def state_space(inputs, step_size, decay_rate, in_coef, out_coef):
    length, head_count, head_width = inputs.shape
    state_dim = in_coef.shape[1]
    blocks = length // SPAN
    blocked = inputs.reshape(blocks, SPAN, head_count, head_width)
    step_blk = step_size.reshape(blocks, SPAN, head_count)
    in_blk = in_coef.reshape(blocks, SPAN, state_dim)
    out_blk = out_coef.reshape(blocks, SPAN, state_dim)
    running = jnp.cumsum(step_blk * decay_rate, axis=1)
    position = jnp.arange(SPAN)
    causal = (position[:, None] >= position[None, :])[None, :, :, None]
    spread = running[:, :, None, :] - running[:, None, :, :]
    decays = jnp.where(causal, jnp.exp(jnp.where(causal, spread, 0.0)), 0.0)
    scores = jnp.einsum('ctn,csn->cts', out_blk, in_blk, precision=HIGHEST)
    mixing = scores[:, :, :, None] * decays * step_blk[:, None, :, :]
    within = jnp.einsum('ctsh,cshp->cthp', mixing, blocked, precision=HIGHEST)
    to_end = jnp.exp(running[:, -1:, :] - running) * step_blk
    weighted = blocked * to_end[:, :, :, None]
    states = jnp.einsum('csn,cshp->chpn', in_blk, weighted, precision=HIGHEST)
    block_decay = jnp.exp(running[:, -1, :])

    def advance(carried, element):
        fresh, factor = element
        return (carried * factor[:, None, None] + fresh, carried)
    initial = jnp.zeros((head_count, head_width, state_dim), jnp.float32)
    _, entering = lax.scan(advance, initial, (states, block_decay))
    from_past = jnp.einsum('ctn,chpn->cthp', out_blk, entering, precision=HIGHEST)
    from_past = from_past * jnp.exp(running)[:, :, :, None]
    return (within + from_past).reshape(length, head_count, head_width)

def mixer(conv_x, conv_coef, gate_in, dt_raw, dt_shift, log_rate, skip_coef):
    length = conv_x.shape[0]
    head_count = dt_raw.shape[1]
    inputs = conv_x.reshape(length, head_count, -1)
    step_size = jax.nn.softplus(dt_raw + dt_shift)
    decay_rate = -jnp.exp(log_rate)
    half = conv_coef.shape[1] // 2
    mixed = state_space(inputs, step_size, decay_rate, conv_coef[:, :half], conv_coef[:, half:])
    mixed = mixed + skip_coef[None, :, None] * inputs
    return mixed.reshape(length, -1) * jax.nn.silu(gate_in)

def reference(hidden, cotangent, norm_gain, in_proj, conv_weight, conv_bias, dt_bias, a_log, d_skip, gate_gain, out_proj):

    def one_sequence(rows, incoming):
        stored = []
        stream = rows
        for layer_idx in range(LAYERS):
            normed = row_norm(stream, norm_gain[layer_idx].astype(jnp.float32)).astype(jnp.bfloat16)
            projected = jnp.dot(normed, in_proj[layer_idx], preferred_element_type=jnp.float32).astype(jnp.bfloat16)
            gate_in = projected[:, :INNER]
            signal = projected[:, INNER:2 * INNER + 2 * STATE].astype(jnp.float32)
            dt_raw = projected[:, 2 * INNER + 2 * STATE:]
            kernel = conv_weight[layer_idx].astype(jnp.float32)
            offset = conv_bias[layer_idx].astype(jnp.float32)
            conv_out = causal_conv(signal, kernel, offset).astype(jnp.bfloat16)
            mix_args = (conv_out[:, :INNER].astype(jnp.float32), conv_out[:, INNER:].astype(jnp.float32), gate_in.astype(jnp.float32), dt_raw.astype(jnp.float32), dt_bias[layer_idx], a_log[layer_idx], d_skip[layer_idx])
            gated = mixer(*mix_args).astype(jnp.bfloat16)
            gnormed = row_norm(gated.astype(jnp.float32), gate_gain[layer_idx].astype(jnp.float32)).astype(jnp.bfloat16)
            stored.append((stream, normed, signal, kernel, offset, mix_args, gated, gnormed))
            stream = stream + jnp.dot(gnormed, out_proj[layer_idx], preferred_element_type=jnp.float32)
        upstream = incoming
        results = [None] * LAYERS
        for layer_idx in reversed(range(LAYERS)):
            stream_in, normed, signal, kernel, offset, mix_args, gated, gnormed = stored[layer_idx]
            upstream_b = upstream.astype(jnp.bfloat16)
            grad_out = jnp.dot(gnormed.T, upstream_b, preferred_element_type=jnp.float32)
            d_gnormed = jnp.dot(upstream_b, out_proj[layer_idx].T, preferred_element_type=jnp.float32)
            _, pull_gate = jax.vjp(row_norm, gated.astype(jnp.float32), gate_gain[layer_idx].astype(jnp.float32))
            d_gated, grad_ggain = pull_gate(d_gnormed)
            d_gated = d_gated.astype(jnp.bfloat16)
            _, pull_mix = jax.vjp(mixer, *mix_args)
            d_convx, d_coef, d_gate, d_steps, grad_shift, grad_rate, grad_skip = pull_mix(d_gated.astype(jnp.float32))
            _, pull_conv = jax.vjp(causal_conv, signal, kernel, offset)
            d_signal, grad_kernel, grad_offset = pull_conv(jnp.concatenate([d_convx, d_coef], axis=1))
            d_projected = jnp.concatenate([d_gate, d_signal, d_steps], axis=1).astype(jnp.bfloat16)
            grad_in = jnp.dot(normed.T, d_projected, preferred_element_type=jnp.float32)
            d_normed = jnp.dot(d_projected, in_proj[layer_idx].T, preferred_element_type=jnp.float32)
            _, pull_norm = jax.vjp(row_norm, stream_in, norm_gain[layer_idx].astype(jnp.float32))
            d_stream, grad_ngain = pull_norm(d_normed)
            upstream = upstream + d_stream
            results[layer_idx] = (grad_ngain, grad_in, grad_kernel, grad_offset, grad_shift, grad_rate, grad_skip, grad_ggain, grad_out)
        stacked = tuple((jnp.stack([results[i][k] for i in range(LAYERS)]) for k in range(9)))
        return (stream, upstream, stacked)
    rows_all = hidden.reshape(SEQS, SEQLEN, D)
    cot_all = cotangent.reshape(SEQS, SEQLEN, D)
    shapes = [(LAYERS, D), (LAYERS, D, PROJ), (LAYERS, CONV, CONV_CH), (LAYERS, CONV_CH), (LAYERS, HEADS), (LAYERS, HEADS), (LAYERS, HEADS), (LAYERS, INNER), (LAYERS, INNER, D)]
    initial = tuple((jnp.zeros(shape, jnp.float32) for shape in shapes))

    def accumulate(totals, element):
        result_rows, result_grad, parts_seq = one_sequence(element[0], element[1])
        return (tuple((a + b for a, b in zip(totals, parts_seq))), (result_rows, result_grad))
    totals, (outputs, grads) = lax.scan(accumulate, initial, (rows_all, cot_all))
    return (outputs.reshape(TOKENS, D), grads.reshape(TOKENS, D), totals[0], totals[1], totals[2], totals[3], totals[4], totals[5], totals[6], totals[7], totals[8])
```

```python
import functools

import jax
import jax.numpy as jnp
from jax import lax
from jax.experimental import pallas as pl
from jax.experimental.pallas import tpu as pltpu
from jax.sharding import PartitionSpec as P

STATE = 128
CHUNK = 128
HEAD = 64
F32 = jnp.float32
BF16 = jnp.bfloat16
HIGHEST = lax.Precision.HIGHEST
VMEM_LIMIT = 56 * 1024 * 1024


def mm(a, b):
    return lax.dot_general(a, b, (((1,), (0,)), ((), ())), preferred_element_type=F32)


def mm_nt(a, b):
    return lax.dot_general(a, b, (((1,), (1,)), ((), ())), preferred_element_type=F32)


def mm_tn(a, b):
    return lax.dot_general(a, b, (((0,), (0,)), ((), ())), preferred_element_type=F32)


def iota(shape, dim):
    return lax.broadcasted_iota(jnp.int32, shape, dim)


def sigmoid(v):
    return 1.0 / (1.0 + jnp.exp(-v))


def spread(cols, heads):
    rows = cols.shape[0]
    lane = iota((rows, 2 * HEAD), 1)
    out = []
    for h in range(0, heads, 2):
        lo = jnp.broadcast_to(cols[:, h : h + 1], (rows, 2 * HEAD))
        hi = jnp.broadcast_to(cols[:, h + 1 : h + 2], (rows, 2 * HEAD))
        out.append(jnp.where(lane < HEAD, lo, hi))
    return jnp.concatenate(out, axis=1)


def spread_rows(row, heads, width):
    return jnp.concatenate(
        [jnp.broadcast_to(row[:, h : h + 1], (HEAD, width)) for h in range(heads)], axis=0
    )


def conv_pre(window, conv_ref, rows):
    pre = jnp.broadcast_to(conv_ref[4:5, :], (rows, window.shape[1]))
    for k in range(4):
        pre = pre + conv_ref[k : k + 1, :] * window[5 + k : 5 + k + rows, :]
    return pre


def steps_of(dt_raw, par_ref):
    v = dt_raw + par_ref[0:1, :]
    step = jnp.maximum(v, 0.0) + jnp.log1p(jnp.exp(-jnp.abs(v)))
    decay = step * par_ref[1:2, :]
    n = dt_raw.shape[0]
    tri = (iota((n, n), 0) >= iota((n, n), 1)).astype(F32)
    run = lax.dot_general(
        tri, decay, (((1,), (0,)), ((), ())), precision=HIGHEST, preferred_element_type=F32
    )
    return step, run


def k_conv(heads, q_ref, proj_ref, halo_ref, conv_ref, par_ref, cx_ref, step_ref, run_ref,
           sloc_ref, gcum_ref, sfin_ref, win, state, cum):
    c = pl.program_id(0)
    inner = heads * HEAD
    n = CHUNK
    chan = inner + 2 * STATE

    @pl.when(c == 0)
    def _():
        win[0:8, :] = halo_ref[...]
        state[...] = jnp.zeros_like(state)
        cum[...] = jnp.zeros_like(cum)

    @pl.when(c > 0)
    def _():
        win[0:8, :] = win[n : n + 8, :]

    win[8:, :] = proj_ref[:, inner : inner + chan].astype(F32)
    pre = conv_pre(win, conv_ref, n)
    act = (pre * sigmoid(pre)).astype(BF16)
    cx_ref[...] = act
    step, run = steps_of(proj_ref[:, inner + chan :].astype(F32), par_ref)
    step_ref[...] = step
    run_ref[...] = run
    sloc_ref[0] = state[...]
    gcum_ref[...] = jnp.broadcast_to(cum[...], (8, 128))
    last = run[n - 1 : n, :]
    weight = jnp.exp(last - run) * step
    xw = (act[:, :inner].astype(F32) * spread(weight, heads)).astype(BF16)
    fresh = mm_tn(xw, act[:, inner : inner + STATE])
    state[...] = state[...] * spread_rows(jnp.exp(last), heads, STATE) + fresh
    cum[...] = cum[...] + last
    sfin_ref[...] = state[...]


def k_within(heads, q_ref, cx_ref, step_ref, run_ref, yw_ref):
    n = CHUNK
    inner = heads * HEAD
    b = cx_ref[:, inner : inner + STATE]
    cc = cx_ref[:, inner + STATE :]
    causal = iota((n, n), 0) >= iota((n, n), 1)
    scores = mm_nt(cc, b)
    run = run_ref[...]
    run_t = jnp.transpose(run)
    step_t = jnp.transpose(step_ref[...])
    lane = iota((n, 2 * HEAD), 1)
    for h in range(0, heads, 2):
        mats = []
        for i in (h, h + 1):
            diff = jnp.broadcast_to(run[:, i : i + 1], (n, n)) - run_t[i : i + 1, :]
            dec = jnp.exp(jnp.where(causal, diff, -1e30))
            mats.append((scores * dec * step_t[i : i + 1, :]).astype(BF16))
        xp = cx_ref[:, h * HEAD : (h + 2) * HEAD]
        zero = jnp.zeros_like(xp)
        stacked = jnp.concatenate(
            [jnp.where(lane < HEAD, xp, zero), jnp.where(lane < HEAD, zero, xp)], axis=0
        )
        yw_ref[:, h * HEAD : (h + 2) * HEAD] = mm(jnp.concatenate(mats, axis=1), stacked)


def k_gate(heads, q_ref, yw_ref, cx_ref, proj_ref, run_ref, sloc_ref, gcum_ref, sin_ref, par_ref,
           y_ref, gated_ref, ssq_ref, *, pieces_rows):
    c = pl.program_id(0)
    n = CHUNK
    inner = heads * HEAD
    cc = cx_ref[:, inner + STATE :]
    grow = jnp.exp(gcum_ref[0:1, :])
    ent = (sloc_ref[0] + sin_ref[...] * spread_rows(grow, heads, STATE)).astype(BF16)
    yi = mm_nt(cc, ent)
    dvec = spread(jnp.broadcast_to(par_ref[2:3, :], (8, 128)), heads)[0:1, :]
    y = yw_ref[...] + spread(jnp.exp(run_ref[...]), heads) * yi
    y = y + dvec * cx_ref[:, :inner].astype(F32)
    y_ref[...] = y.astype(BF16)
    z = proj_ref[...].astype(F32)
    gated = (y * (z * sigmoid(z))).astype(BF16)
    gated_ref[...] = gated
    gf = gated.astype(F32)
    total = jnp.sum(gf * gf, axis=1, keepdims=True)
    flat = jnp.transpose(jnp.broadcast_to(total, (n, n)))[0:1, :]
    blk = row_block(c, q_ref, pieces_rows)
    ssq_ref[pl.ds(blk, 1), :] = flat


def row_block(c, q_ref, pieces_rows):
    per = pieces_rows // CHUNK
    return ((c // per) ^ q_ref[0]) * per + c % per


def k_pre(heads, q_ref, dgn_ref, gated_ref, grs_ref, srow_ref, gain_ref, z_ref, cx_ref, run_ref,
          gcum_ref, dg_ref, dsin_ref):
    c = pl.program_id(0)
    inner = heads * HEAD
    grs = grs_ref[...]
    gated = gated_ref[...].astype(F32)
    dg = grs * gain_ref[...] * dgn_ref[...] - gated * (grs * grs * grs * srow_ref[...])
    dg = dg.astype(BF16)
    dg_ref[...] = dg
    z = z_ref[...].astype(F32)
    dy = dg.astype(F32) * (z * sigmoid(z))
    cum = jnp.exp(run_ref[...] + gcum_ref[0:1, :])
    dyw = (dy * spread(cum, heads)).astype(BF16)
    add = mm_tn(dyw, cx_ref[:, inner + STATE :])

    @pl.when(c == 0)
    def _():
        dsin_ref[...] = add

    @pl.when(c > 0)
    def _():
        dsin_ref[...] = dsin_ref[...] + add


def fold8(v):
    return jnp.sum(v.reshape(v.shape[0] // 8, 8, v.shape[1]), axis=0)


def k_back(heads, last_chunk, q_ref, proj_ref, prev_ref, halo_ref, cx_ref, y_ref, dg_ref, step_ref,
           run_ref, sloc_ref, gcum_ref, sin_ref, dsout_ref, conv_ref, par_ref,
           dproj_ref, dlast_ref, dfirst_ref, gconv_ref, ghead_ref, gskip_ref,
           win, dwin, dstate, gacc, hacc, sacc):
    i = pl.program_id(0)
    c = last_chunk - i
    n = CHUNK
    inner = heads * HEAD
    chan = inner + 2 * STATE

    @pl.when(i == 0)
    def _():
        dstate[...] = dsout_ref[...]
        dwin[n : n + 8, :] = jnp.zeros((8, chan), F32)
        gacc[...] = jnp.zeros_like(gacc)
        hacc[...] = jnp.zeros_like(hacc)
        sacc[...] = jnp.zeros_like(sacc)

    @pl.when(i > 0)
    def _():
        dwin[n : n + 8, :] = dwin[0:8, :]

    @pl.when(c == 0)
    def _():
        win[0:8, :] = halo_ref[...]

    @pl.when(c > 0)
    def _():
        win[0:8, :] = prev_ref[8:16, inner : inner + chan].astype(F32)

    win[8:, :] = proj_ref[:, inner : inner + chan].astype(F32)

    z = proj_ref[:, :inner].astype(F32)
    sz = sigmoid(z)
    dg = dg_ref[...].astype(F32)
    dproj_ref[:, :inner] = (dg * y_ref[...].astype(F32) * (sz * (1.0 + z * (1.0 - sz)))).astype(BF16)
    dy = dg * (z * sz)
    dyb = dy.astype(BF16)
    x = cx_ref[:, :inner]
    xf = x.astype(F32)
    b = cx_ref[:, inner : inner + STATE]
    cc = cx_ref[:, inner + STATE :]
    sacc[...] += fold8(dy * xf)

    run = run_ref[...]
    step = step_ref[...]
    run_t = jnp.transpose(run)
    step_t = jnp.transpose(step)
    last = run[n - 1 : n, :]
    causal = iota((n, n), 0) >= iota((n, n), 1)
    lane = iota((n, 2 * HEAD), 1)
    lane128 = iota((n, 128), 1)
    scores = mm_nt(cc, b)
    dscores = jnp.zeros((n, n), F32)
    rows_acc = jnp.zeros((n, 128), F32)
    cols = []
    dxs = []
    for h in range(0, heads, 2):
        sl = slice(h * HEAD, (h + 2) * HEAD)
        dyp = dyb[:, sl]
        zero = jnp.zeros_like(dyp)
        dy2 = jnp.concatenate(
            [jnp.where(lane < HEAD, dyp, zero), jnp.where(lane < HEAD, zero, dyp)], axis=0
        )
        dm2 = mm_nt(dy2, x[:, sl])
        mats = []
        for j in (0, 1):
            k = h + j
            diff = jnp.broadcast_to(run[:, k : k + 1], (n, n)) - run_t[k : k + 1, :]
            dec = jnp.exp(jnp.where(causal, diff, -1e30))
            srow = step_t[k : k + 1, :]
            ms = scores * dec
            dm = dm2[j * n : (j + 1) * n, :]
            mats.append((ms * srow).astype(BF16))
            dscores = dscores + dm * (dec * srow)
            e = dm * ms
            cols.append(jnp.sum(e, axis=0, keepdims=True))
            rs = jnp.sum(e * srow, axis=1, keepdims=True)
            rows_acc = jnp.where(lane128 == k, rs, rows_acc)
        dxs.append(mm_tn(jnp.concatenate(mats, axis=0), dy2))
    dx = jnp.concatenate(dxs, axis=1)
    cols_t = jnp.concatenate(cols + [jnp.zeros((128 - heads, n), F32)], axis=0)
    col = jnp.transpose(cols_t)

    grow = jnp.exp(gcum_ref[0:1, :])
    ent_f = sloc_ref[0] + sin_ref[...] * spread_rows(grow, heads, STATE)
    ent = ent_f.astype(BF16)
    dst = dstate[...]
    dstb = dst.astype(BF16)
    erun = jnp.exp(run)
    weight_n = jnp.exp(last - run)
    weight = weight_n * step
    pick = (iota((inner, 128), 0) // HEAD == iota((inner, 128), 1)).astype(BF16)
    dyw = dy * spread(erun, heads)
    dywb = dyw.astype(BF16)
    yi = mm_nt(cc, ent)
    rows_acc = rows_acc + mm((dyw * yi).astype(BF16), pick)
    bds = mm_nt(b, dstb)
    wexp = spread(weight, heads)
    gsum = mm((xf * bds).astype(BF16), pick)
    dx = dx + wexp * bds
    dvec = spread(jnp.broadcast_to(par_ref[2:3, :], (8, 128)), heads)[0:1, :]
    dx = dx + dvec * dy
    dscb = dscores.astype(BF16)
    dc = mm(dscb, b) + mm(dywb, ent)
    db = mm_tn(dscb, cc) + mm((xf * wexp).astype(BF16), dstb)

    prod = dst * ent_f
    lane1 = iota((1, 128), 1)
    inner_dot = jnp.zeros((1, 128), F32)
    for k in range(heads):
        part = jnp.sum(prod[k * HEAD : (k + 1) * HEAD, :], axis=0, keepdims=True)
        part = jnp.sum(part, axis=1, keepdims=True)
        inner_dot = jnp.where(lane1 == k, part, inner_dot)
    wg = weight * gsum
    d_last = jnp.exp(last) * inner_dot + jnp.sum(wg, axis=0, keepdims=True)
    d_run = rows_acc - step * col - wg
    d_run = d_run + jnp.where(iota((n, 128), 0) == n - 1, d_last, 0.0)
    d_step = col + weight_n * gsum
    triu = (iota((n, n), 0) <= iota((n, n), 1)).astype(F32)
    d_a = lax.dot_general(
        triu, d_run, (((1,), (0,)), ((), ())), precision=HIGHEST, preferred_element_type=F32
    )
    rate = par_ref[1:2, :]
    d_step = d_step + rate * d_a
    d_dt = d_step * sigmoid(proj_ref[:, inner + chan :].astype(F32) + par_ref[0:1, :])
    d_dt = jnp.where(lane128 < heads, d_dt, 0.0)
    dproj_ref[:, inner + chan :] = d_dt.astype(BF16)
    hacc[0:8, :] += fold8(d_dt)
    hacc[8:16, :] += fold8(jnp.where(lane128 < heads, d_a * step * rate, 0.0))

    dstate[...] = dst * spread_rows(jnp.exp(last), heads, STATE) + mm_tn(dywb, cc)

    pre = conv_pre(win, conv_ref, n)
    sp = sigmoid(pre)
    dpre = jnp.concatenate([dx, db, dc], axis=1) * (sp * (1.0 + pre * (1.0 - sp)))
    dwin[0:n, :] = dpre
    for k in range(4):
        gacc[8 * k : 8 * k + 8, :] += fold8(dpre * win[5 + k : 5 + k + n, :])
    gacc[32:40, :] += fold8(dpre)
    dxbc = jnp.zeros((n, chan), F32)
    for k in range(4):
        dxbc = dxbc + conv_ref[k : k + 1, :] * dwin[3 - k : 3 - k + n, :]
    dproj_ref[:, inner : inner + chan] = dxbc.astype(BF16)

    @pl.when(i == 0)
    def _():
        dlast_ref[...] = dxbc[n - 8 :, :]

    dfirst_ref[...] = dpre[0:8, :]
    gconv_ref[...] = gacc[...]
    ghead_ref[...] = hacc[...]
    gskip_ref[...] = sacc[...]


def call(body, grid, in_specs, out_specs, out_shape, scratch, interpret, cost, *args):
    return pl.pallas_call(
        body,
        grid_spec=pltpu.PrefetchScalarGridSpec(
            num_scalar_prefetch=1,
            grid=grid,
            in_specs=in_specs,
            out_specs=out_specs,
            scratch_shapes=scratch,
        ),
        out_shape=out_shape,
        compiler_params=pltpu.CompilerParams(
            dimension_semantics=("arbitrary",), vmem_limit_bytes=VMEM_LIMIT
        ),
        cost_estimate=cost,
        interpret=interpret,
    )(*args)


def sds(shape, dtype):
    return jax.ShapeDtypeStruct(shape, dtype)


def forward_states(q, proj, halo, conv, par, heads, piece, interpret=False):
    rows, width = proj.shape
    inner = heads * HEAD
    chan = inner + 2 * STATE
    chunks = rows // CHUNK
    at = lambda c, q: (row_block(c, q, piece), 0)
    whole = lambda c, q: (0, 0)
    cost = pl.CostEstimate(flops=2 * rows * inner * STATE, transcendentals=rows * chan,
                           bytes_accessed=rows * (2 * width + 2 * chan + 1024) + 4 * chunks * inner * STATE)
    return call(
        functools.partial(k_conv, heads),
        (chunks,),
        [
            pl.BlockSpec((CHUNK, width), at),
            pl.BlockSpec((8, chan), whole),
            pl.BlockSpec((8, chan), whole),
            pl.BlockSpec((8, 128), whole),
        ],
        [
            pl.BlockSpec((CHUNK, chan), at),
            pl.BlockSpec((CHUNK, 128), at),
            pl.BlockSpec((CHUNK, 128), at),
            pl.BlockSpec((1, inner, STATE), lambda c, q: (c, 0, 0)),
            pl.BlockSpec((8, 128), lambda c, q: (c, 0)),
            pl.BlockSpec((inner, STATE), whole),
        ],
        [
            sds((rows, chan), BF16),
            sds((rows, 128), F32),
            sds((rows, 128), F32),
            sds((chunks, inner, STATE), F32),
            sds((8 * chunks, 128), F32),
            sds((inner, STATE), F32),
        ],
        [
            pltpu.VMEM((CHUNK + 8, chan), F32),
            pltpu.VMEM((inner, STATE), F32),
            pltpu.VMEM((1, 128), F32),
        ],
        interpret,
        cost,
        q, proj, halo, conv, par,
    )


def forward_within(q, cx, step, run, heads, piece, interpret=False):
    rows, chan = cx.shape
    inner = heads * HEAD
    at = lambda c, q: (row_block(c, q, piece), 0)
    cost = pl.CostEstimate(flops=4 * rows * inner * CHUNK, transcendentals=rows * CHUNK * heads,
                           bytes_accessed=rows * (2 * chan + 1024 + 4 * inner))
    return call(
        functools.partial(k_within, heads),
        (rows // CHUNK,),
        [pl.BlockSpec((CHUNK, chan), at), pl.BlockSpec((CHUNK, 128), at), pl.BlockSpec((CHUNK, 128), at)],
        [pl.BlockSpec((CHUNK, inner), at)],
        [sds((rows, inner), F32)],
        [],
        interpret,
        cost,
        q, cx, step, run,
    )[0]


def forward_gate(q, yw, cx, proj, run, sloc, gcum, sin, par, heads, piece, interpret=False):
    rows, chan = cx.shape
    inner = heads * HEAD
    chunks = rows // CHUNK
    at = lambda c, q: (row_block(c, q, piece), 0)
    whole = lambda c, q: (0, 0)
    cost = pl.CostEstimate(flops=2 * rows * inner * STATE, transcendentals=rows * inner,
                           bytes_accessed=rows * (10 * inner + 2 * chan + 512) + 4 * chunks * inner * STATE)
    return call(
        functools.partial(k_gate, heads, pieces_rows=piece),
        (chunks,),
        [
            pl.BlockSpec((CHUNK, inner), at),
            pl.BlockSpec((CHUNK, chan), at),
            pl.BlockSpec((CHUNK, inner), at),
            pl.BlockSpec((CHUNK, 128), at),
            pl.BlockSpec((1, inner, STATE), lambda c, q: (c, 0, 0)),
            pl.BlockSpec((8, 128), lambda c, q: (c, 0)),
            pl.BlockSpec((inner, STATE), whole),
            pl.BlockSpec((8, 128), whole),
        ],
        [
            pl.BlockSpec((CHUNK, inner), at),
            pl.BlockSpec((CHUNK, inner), at),
            pl.BlockSpec((chunks, 128), whole),
        ],
        [sds((rows, inner), BF16), sds((rows, inner), BF16), sds((chunks, 128), F32)],
        [],
        interpret,
        cost,
        q, yw, cx, proj, run, sloc, gcum, sin, par,
    )


def backward_pre(q, dgn, gated, grs, srow, gain, proj, cx, run, gcum, heads, piece, interpret=False):
    rows, chan = cx.shape
    inner = heads * HEAD
    chunks = rows // CHUNK
    at = lambda c, q: (row_block(c, q, piece), 0)
    whole = lambda c, q: (0, 0)
    cost = pl.CostEstimate(flops=2 * rows * inner * STATE, transcendentals=rows * inner,
                           bytes_accessed=rows * (10 * inner + 2 * chan + 512))
    return call(
        functools.partial(k_pre, heads),
        (chunks,),
        [
            pl.BlockSpec((CHUNK, inner), at),
            pl.BlockSpec((CHUNK, inner), at),
            pl.BlockSpec((CHUNK, 1), at),
            pl.BlockSpec((CHUNK, 1), at),
            pl.BlockSpec((1, inner), whole),
            pl.BlockSpec((CHUNK, inner), at),
            pl.BlockSpec((CHUNK, chan), at),
            pl.BlockSpec((CHUNK, 128), at),
            pl.BlockSpec((8, 128), lambda c, q: (c, 0)),
        ],
        [pl.BlockSpec((CHUNK, inner), at), pl.BlockSpec((inner, STATE), whole)],
        [sds((rows, inner), BF16), sds((inner, STATE), F32)],
        [],
        interpret,
        cost,
        q, dgn, gated, grs, srow, gain, proj, cx, run, gcum,
    )


def backward_main(q, proj, halo, cx, y, dg, step, run, sloc, gcum, sin, dsout, conv, par, heads,
                  piece, interpret=False):
    rows, width = proj.shape
    inner = heads * HEAD
    chan = inner + 2 * STATE
    chunks = rows // CHUNK
    last = chunks - 1
    at = lambda i, q: (row_block(last - i, q, piece), 0)

    def before(i, q):
        c = jnp.maximum(last - i - 1, 0)
        return (row_block(c, q, piece) * (CHUNK // 16) + CHUNK // 16 - 1, 0)

    whole = lambda i, q: (0, 0)
    cost = pl.CostEstimate(flops=12 * rows * inner * STATE, transcendentals=rows * CHUNK * heads,
                           bytes_accessed=rows * (4 * width + 2 * chan + 4 * inner + 1024) + 4 * chunks * inner * STATE)
    return call(
        functools.partial(k_back, heads, last),
        (chunks,),
        [
            pl.BlockSpec((CHUNK, width), at),
            pl.BlockSpec((16, width), before),
            pl.BlockSpec((8, chan), whole),
            pl.BlockSpec((CHUNK, chan), at),
            pl.BlockSpec((CHUNK, inner), at),
            pl.BlockSpec((CHUNK, inner), at),
            pl.BlockSpec((CHUNK, 128), at),
            pl.BlockSpec((CHUNK, 128), at),
            pl.BlockSpec((1, inner, STATE), lambda i, q: (last - i, 0, 0)),
            pl.BlockSpec((8, 128), lambda i, q: (last - i, 0)),
            pl.BlockSpec((inner, STATE), whole),
            pl.BlockSpec((inner, STATE), whole),
            pl.BlockSpec((8, chan), whole),
            pl.BlockSpec((8, 128), whole),
        ],
        [
            pl.BlockSpec((CHUNK, width), at),
            pl.BlockSpec((8, chan), whole),
            pl.BlockSpec((8, chan), whole),
            pl.BlockSpec((40, chan), whole),
            pl.BlockSpec((16, 128), whole),
            pl.BlockSpec((8, inner), whole),
        ],
        [
            sds((rows, width), BF16),
            sds((8, chan), F32),
            sds((8, chan), F32),
            sds((40, chan), F32),
            sds((16, 128), F32),
            sds((8, inner), F32),
        ],
        [
            pltpu.VMEM((CHUNK + 8, chan), F32),
            pltpu.VMEM((CHUNK + 8, chan), F32),
            pltpu.VMEM((inner, STATE), F32),
            pltpu.VMEM((40, chan), F32),
            pltpu.VMEM((16, 128), F32),
            pltpu.VMEM((8, inner), F32),
        ],
        interpret,
        cost,
        q, proj, proj, halo, cx, y, dg, step, run, sloc, gcum, sin, dsout, conv, par,
    )


SEQLEN = 2048
GROUP = 4
EPS = 1e-05


def bits_of(n):
    return [1 << i for i in range(n.bit_length() - 1)]


def swap(x, bit):
    n = x.shape[0]
    y = x.reshape((n // (2 * bit), 2, bit) + x.shape[1:])
    return jnp.concatenate([y[:, 1:], y[:, :1]], axis=1).reshape(x.shape)


def xor_order(x, index, axis=0):
    x = jnp.moveaxis(x, axis, 0)
    for bit in bits_of(x.shape[0]):
        x = jnp.where((index & bit) > 0, swap(x, bit), x)
    return jnp.moveaxis(x, 0, axis)


def pick(x, index, axis):
    return lax.dynamic_index_in_dim(x, index, axis, keepdims=False)


class Plan:
    def __init__(self):
        self.nb = lax.axis_size("batch")
        self.ns = lax.axis_size("seq")
        self.groups = self.ns // GROUP
        b, s = lax.axis_index("batch"), lax.axis_index("seq")
        self.q = s % GROUP
        self.block = b * self.groups + s // GROUP

    def sx(self, x, k):
        return lax.ppermute(x, "seq", [(i, i ^ k) for i in range(self.ns)])

    def bx(self, x, k):
        return lax.ppermute(x, "batch", [(i, i ^ k) for i in range(self.nb)])

    def shift(self, x, step, per_seq):
        pairs = []
        for i in range(self.ns):
            place = (i // GROUP) % per_seq + step
            if 0 <= place < per_seq:
                pairs.append((i, i + step * GROUP))
        return lax.ppermute(x, "seq", pairs)

    def exchange(self, targets):
        own, near, far, diag = (pick(targets, self.q ^ k, 0) for k in range(GROUP))
        first = self.sx(jnp.stack([near, diag]), 1)
        second = self.sx(jnp.stack([far, first[1]]), 2)
        return jnp.stack([own, first[0], second[0], second[1]])

    def gather_rows(self, x):
        near = self.sx(x, 1)
        far = self.sx(x, 2)
        return jnp.concatenate([x, near, far, self.sx(far, 1)], axis=0)

    def scatter_rows(self, x):
        n = x.shape[0] // GROUP
        part = x.reshape(GROUP, n, x.shape[1])
        got = self.sx(jnp.stack([part[1], part[3]]), 1)
        far = part[2].astype(F32) + got[1].astype(F32)
        got2 = self.sx(far.astype(BF16), 2)
        return part[0].astype(F32) + got[0].astype(F32) + got2.astype(F32)

    def group_sum(self, x):
        m = x.shape[0] // GROUP
        for k in (1, 2):
            got = self.sx(x, k).reshape(GROUP, m, x.shape[1])
            x = x + swap(got, k).reshape(x.shape)
        return x

    def all_small(self, x):
        x = x[None]
        place = lax.axis_index("seq")
        for bit in bits_of(self.ns):
            got = self.sx(x, bit)
            up = (place & bit) > 0
            x = jnp.concatenate([jnp.where(up, got, x), jnp.where(up, x, got)], axis=0)
        place = lax.axis_index("batch")
        for bit in bits_of(self.nb):
            got = self.bx(x, bit)
            up = (place & bit) > 0
            x = jnp.concatenate([jnp.where(up, got, x), jnp.where(up, x, got)], axis=0)
        return x

    def batch_gather(self, x):
        half = x.shape[0] // 2
        bits = bits_of(self.nb)
        out = []
        for part, order in ((x[:half], bits), (x[half:], bits[::-1])):
            have = {0: part}
            for bit in order:
                keys = sorted(have)
                got = self.bx(jnp.concatenate([have[k] for k in keys], axis=0), bit)
                for i, k in enumerate(keys):
                    have[k ^ bit] = got[i * half : (i + 1) * half]
            out.append(have)
        return [[out[0][k], out[1][k]] for k in range(self.nb)]

    def gather_blocks(self, x):
        per_group = [self.batch_gather(x)]
        have = [x]
        for bit in bits_of(self.groups):
            got = self.sx(jnp.stack(have), GROUP * bit)
            fresh = [got[i] for i in range(len(have))]
            have += fresh
            per_group += [self.batch_gather(f) for f in fresh]
        pieces = []
        for k in range(self.nb):
            for g in range(self.groups):
                pieces += per_group[g][k]
        return jnp.concatenate(pieces, axis=0)

    def batch_reduce(self, blocks):
        half = blocks[0].shape[0] // 2
        bits = bits_of(self.nb)
        out = []
        for part, order in ((0, bits), (1, bits[::-1])):
            have = {k: v[part * half : (part + 1) * half] for k, v in enumerate(blocks)}
            for bit in order:
                keys = sorted(k for k in have if k & bit)
                got = self.bx(jnp.concatenate([have[k] for k in keys], axis=0), bit)
                left = {}
                for i, k in enumerate(keys):
                    mine = have[k ^ bit].astype(F32)
                    left[k ^ bit] = (mine + got[i * half : (i + 1) * half].astype(F32)).astype(BF16)
                have = left
            out.append(have[0])
        return jnp.concatenate(out, axis=0)

    def reduce_blocks(self, x):
        n = x.shape[0] // (self.nb * self.groups)
        part = x.reshape(self.nb, self.groups, n, x.shape[1])
        sums = {}
        for g in reversed(range(self.groups)):
            sums[g] = self.batch_reduce([part[k, g] for k in range(self.nb)])
        for bit in reversed(bits_of(self.groups)):
            keys = sorted(k for k in sums if k & bit)
            got = self.sx(jnp.stack([sums[k] for k in keys]), GROUP * bit)
            sums = {
                k ^ bit: (sums[k ^ bit].astype(F32) + got[i].astype(F32)).astype(BF16)
                for i, k in enumerate(keys)
            }
        return sums[0]


def split3(x):
    hi = x.astype(BF16)
    rest = x - hi.astype(F32)
    mid = rest.astype(BF16)
    return jnp.stack([hi, mid, (rest - mid.astype(F32)).astype(BF16)], axis=-1)


def local(hidden, cotangent, norm_gain, in_proj, conv_weight, conv_bias, dt_bias, a_log, d_skip,
          gate_gain, out_proj, interpret=False):
    plan = Plan()
    nb, ns, q, block = plan.nb, plan.ns, plan.q, plan.block
    devices = nb * ns
    blocks = nb * plan.groups
    layers, d_rows, cols = in_proj.shape
    rows, width = hidden.shape
    all_rows = GROUP * rows
    per_seq = SEQLEN // all_rows
    inner_all = gate_gain.shape[1] * devices
    heads_all = dt_bias.shape[1] * ns
    heads = heads_all // GROUP
    inner = heads * HEAD
    coef = 2 * STATE
    chan = inner + coef
    main = 2 * inner + coef
    wide = -(-(main + heads) // 128) * 128
    if wide == main:
        wide += 128
    conv_loc = conv_bias.shape[1]
    taps = conv_weight.shape[1]
    hps = dt_bias.shape[1]
    gate_loc = gate_gain.shape[1]
    out_rows = out_proj.shape[1]
    direct_out = out_rows == HEAD
    qa = q.reshape(1).astype(jnp.int32)

    small = []
    for l in range(layers):
        small.append(jnp.concatenate([
            norm_gain[l],
            conv_weight[l].reshape(-1),
            conv_bias[l],
            gate_gain[l],
            split3(jnp.stack([dt_bias[l], a_log[l], d_skip[l]])).reshape(-1),
        ]))
    count = small[0].shape[0]
    padded = -(-count // 128) * 128
    small = jnp.stack([jnp.pad(v, (0, padded - count)) for v in small])
    small = plan.all_small(small.reshape(-1, 128)).reshape(devices, layers, padded)

    def small_of(l):
        v = small[:, l]
        at = 0
        gain = v[:, at : at + d_rows].reshape(-1)
        at += d_rows
        cw = v[:, at : at + taps * conv_loc].reshape(devices, taps, conv_loc)
        cw = jnp.transpose(cw, (1, 0, 2)).reshape(taps, -1)
        at += taps * conv_loc
        cb = v[:, at : at + conv_loc].reshape(1, -1)
        at += conv_loc
        gg = v[:, at : at + gate_loc].reshape(heads, GROUP, HEAD)
        gg = pick(gg, q, 1).reshape(1, inner).astype(F32)
        at += gate_loc
        hp = v[:ns, at : at + 9 * hps].reshape(ns, 3, hps, 3).astype(F32)
        hp = (hp[..., 0] + hp[..., 1]) + hp[..., 2]
        hp = jnp.transpose(hp, (1, 0, 2)).reshape(3, heads, GROUP)
        hp = pick(hp, q, 2)
        hp = jnp.stack([hp[0], -jnp.exp(hp[1]), hp[2]])
        par = jnp.pad(hp, ((0, 5), (0, 128 - heads)))
        full = jnp.concatenate([cw, cb], axis=0).astype(F32)
        own = pick(full[:, :inner_all].reshape(taps + 1, heads, GROUP, HEAD), q, 2)
        conv = jnp.concatenate([own.reshape(taps + 1, inner), full[:, inner_all:]], axis=1)
        conv = jnp.pad(conv, ((0, 8 - taps - 1), (0, 0)))
        return gain.astype(F32), gg, par, conv

    def gather_in(l):
        w = in_proj[l]

        def by_head(v):
            v = v.reshape(d_rows, heads, GROUP, -1)
            return jnp.transpose(v, (2, 0, 1, 3)).reshape(GROUP, d_rows, -1)

        bc = w[:, 2 * inner_all : 2 * inner_all + coef]
        parts = [
            by_head(w[:, :inner_all]),
            by_head(w[:, inner_all : 2 * inner_all]),
            jnp.broadcast_to(bc[None], (GROUP,) + bc.shape),
            by_head(w[:, 2 * inner_all + coef :]),
            jnp.zeros((GROUP, d_rows, wide - main - heads), BF16),
        ]
        got = xor_order(plan.exchange(jnp.concatenate(parts, axis=2)), q)
        return plan.gather_blocks(got.reshape(GROUP * d_rows, wide))

    def gather_out(l):
        if direct_out:
            w = plan.gather_blocks(out_proj[l]).reshape(blocks, HEAD, width)
            return xor_order(w, block).reshape(inner, width)
        w = lax.all_gather(out_proj[l], ("batch", "seq"), axis=0, tiled=True)
        return pick(w.reshape(heads, GROUP, HEAD, width), q, 1).reshape(inner, width)

    def permuted(v, index):
        n = v.shape[0]
        return xor_order(v.reshape(n, blocks, width // blocks), index, 1).reshape(n, width)

    edge = ((GROUP - 1) ^ q) * rows + rows - 8
    smalls = [small_of(l) for l in range(layers)]
    stored = []
    stream = hidden
    for l in range(layers):
        gain, gg, par, conv = smalls[l]
        w_in = gather_in(l)
        rs = lax.rsqrt(jnp.mean(stream * stream, axis=-1, keepdims=True) + EPS)
        normed = plan.gather_rows(permuted((stream * rs * gain).astype(BF16), block))
        tail = lax.dynamic_slice_in_dim(normed, edge, 8, 0)
        tail = permuted(plan.shift(tail, 1, per_seq), block ^ jnp.maximum(block - 1, 0))
        proj = jnp.dot(normed, w_in, preferred_element_type=F32).astype(BF16)
        halo = jnp.dot(tail, w_in[:, inner:main], preferred_element_type=F32)
        halo = halo.astype(BF16).astype(F32)
        cx, step, run, sloc, gcum, sfin = forward_states(
            qa, proj, halo, conv, par, heads, rows, interpret)
        total = None
        if per_seq > 2:
            total = jnp.exp(gcum[-1] + lax.dynamic_index_in_dim(run, edge + 7, 0, keepdims=False))
            total = jnp.repeat(total[:heads], HEAD)[:, None]
        sin = jnp.zeros_like(sfin)
        for hop in range(per_seq - 1):
            leave = sfin if hop == 0 else sfin + total * sin
            sin = plan.shift(leave.astype(BF16), 1, per_seq).astype(F32)
        yw = forward_within(qa, cx, step, run, heads, rows, interpret)
        y, gated, ssq = forward_gate(
            qa, yw, cx, proj, run, sloc, gcum, sin, par, heads, rows, interpret)
        w_out = gather_out(l)
        grs = lax.rsqrt(plan.group_sum(ssq).reshape(all_rows, 1) / inner_all + EPS)
        gnormed = (gated.astype(F32) * grs * gg).astype(BF16)
        delta = jnp.dot(gnormed, w_out, preferred_element_type=F32).astype(BF16)
        stored.append((stream, rs, normed, w_in, w_out, halo, proj, cx, step, run, sloc, gcum, sin,
                       y, gated, grs, gnormed, total))
        stream = stream + plan.scatter_rows(delta)

    upstream = cotangent
    results = [None] * layers
    for l in reversed(range(layers)):
        gain, gg, par, conv = smalls[l]
        (stream_in, rs, normed, w_in, w_out, halo, proj, cx, step, run, sloc, gcum, sin, y, gated,
         grs, gnormed, total) = stored[l]
        up = plan.gather_rows(upstream.astype(BF16))
        dgn = lax.dot_general(up, w_out, (((1,), (1,)), ((), ())), preferred_element_type=F32)
        srow = jnp.sum(dgn * gg * gated.astype(F32), axis=1).reshape(-1, 128)
        srow = plan.group_sum(srow).reshape(all_rows, 1) / inner_all
        grad_out = lax.dot_general(gnormed, up, (((0,), (0,)), ((), ())), preferred_element_type=F32)
        grad_out = grad_out.astype(BF16)
        dg, dsin = backward_pre(qa, dgn, gated, grs, srow, gg, proj, cx, run, gcum, heads, rows,
                                interpret)
        dsout = jnp.zeros_like(dsin)
        for hop in range(per_seq - 1):
            leave = dsin if hop == 0 else dsin + total * dsout
            dsout = plan.shift(leave.astype(BF16), -1, per_seq).astype(F32)
        dproj, dlast, dfirst, gconv, ghead, gskip = backward_main(
            qa, proj, halo, cx, y, dg, step, run, sloc, gcum, sin, dsout, conv, par, heads, rows,
            interpret)
        after = plan.shift(dfirst, -1, per_seq)
        for k in range(taps - 1):
            dlast = dlast.at[5 + k :].add(conv[k] * after[: 3 - k])
        dproj = lax.dynamic_update_slice(dproj, dlast.astype(BF16), (edge, inner))

        if direct_out:
            grad_out = xor_order(grad_out.reshape(blocks, HEAD, width), block)
            grad_out = plan.reduce_blocks(grad_out.reshape(inner, width)).astype(F32)
        else:
            place = jnp.arange(GROUP)[None, :, None, None] == q
            full = jnp.where(place, grad_out.reshape(heads, 1, HEAD, width), 0)
            grad_out = lax.psum_scatter(full.reshape(inner_all, width), ("batch", "seq"),
                                        scatter_dimension=0, tiled=True).astype(F32)

        gc = jnp.sum(gconv.reshape(taps + 1, 8, chan), axis=1)
        mine = (jnp.arange(GROUP) == q).astype(F32)
        gx = gc[:, :inner].reshape(taps + 1, heads, 1, HEAD) * mine[:, None]
        gc = jnp.concatenate([gx.reshape(taps + 1, inner_all), gc[:, inner:]], axis=1)
        gc = jnp.transpose(gc.reshape(taps + 1, devices, conv_loc), (1, 0, 2)).reshape(devices, -1)
        gh = jnp.sum(ghead.reshape(2, 8, 128), axis=1)[:, :heads]
        gk = jnp.sum(jnp.sum(gskip, axis=0).reshape(heads, HEAD), axis=1)
        gh = jnp.concatenate([gh, gk[None]], axis=0)[:, :, None] * mine
        gh = jnp.transpose(gh.reshape(3, ns, hps), (1, 0, 2)).reshape(1, ns, 3 * hps)
        gh = jnp.broadcast_to(gh, (nb, ns, 3 * hps)).reshape(devices, 3 * hps)
        ride = jnp.concatenate([gc, gh], axis=1)
        lanes = -(-ride.shape[1] // d_rows)
        ride = jnp.pad(ride, ((0, 0), (0, lanes * d_rows - ride.shape[1])))
        ride = xor_order(ride.reshape(blocks, GROUP * d_rows, lanes), block)
        ride = jnp.pad(ride.reshape(width, lanes), ((0, 0), (main + heads, wide - main - heads - lanes)))
        grad_in = lax.dot_general(normed, dproj, (((0,), (0,)), ((), ())), preferred_element_type=F32)
        grad_in = plan.reduce_blocks((grad_in + ride).astype(BF16))
        got = plan.exchange(grad_in.reshape(GROUP, d_rows, wide))
        got = xor_order(got, q).astype(F32)

        def from_heads(v):
            v = v.reshape(GROUP, d_rows, heads, -1)
            return jnp.transpose(v, (1, 2, 0, 3)).reshape(d_rows, -1)

        shared = jnp.sum(got[:, :, 2 * inner : main], axis=0)
        g_in = jnp.concatenate([
            from_heads(got[:, :, :inner]),
            from_heads(got[:, :, inner : 2 * inner]),
            shared,
            from_heads(got[:, :, main : main + heads]),
        ], axis=1)
        back = jnp.sum(got[:, :, main + heads : main + heads + lanes], axis=0).reshape(-1)
        g_conv = back[: (taps + 1) * conv_loc].reshape(taps + 1, conv_loc)
        g_head = back[(taps + 1) * conv_loc : (taps + 1) * conv_loc + 3 * hps].reshape(3, hps)
        g_norm = jnp.sum(g_in * in_proj[l].astype(F32), axis=1) / norm_gain[l].astype(F32)
        g_gate = jnp.sum(grad_out * out_proj[l].astype(F32), axis=1) / gate_gain[l].astype(F32)
        results[l] = (g_norm, g_in, g_conv[:taps], g_conv[taps], g_head[0], g_head[1], g_head[2],
                      g_gate, grad_out)

        dn = lax.dot_general(dproj, w_in, (((1,), (1,)), ((), ())), preferred_element_type=F32)
        dn = permuted(plan.scatter_rows(dn.astype(BF16)), block)
        dn = dn * gain
        mean = jnp.mean(dn * stream_in, axis=-1, keepdims=True)
        upstream = upstream + rs * dn - stream_in * (rs * rs * rs * mean)

    stacked = [jnp.stack([results[l][k] for l in range(layers)]) for k in range(9)]
    return (stream, upstream, *stacked)


def solution(mesh, interpret=False):
    every = ("batch", "seq")
    in_specs = (
        P(every, None), P(every, None), P(None, every), P(None, every, None), P(None, None, every),
        P(None, every), P(None, "seq"), P(None, "seq"), P(None, "seq"), P(None, every),
        P(None, every, None),
    )
    out_specs = (
        P(every, None), P(every, None), P(None, every), P(None, every, None), P(None, None, every),
        P(None, every), P(None, "seq"), P(None, "seq"), P(None, "seq"), P(None, every),
        P(None, every, None),
    )
    body = functools.partial(local, interpret=interpret)
    return jax.shard_map(body, mesh=mesh, in_specs=in_specs, out_specs=out_specs, check_vma=False)
```
